32 devices in a mesh: row: 4 (over y, x), col: 4 (over z), cores: 2 (over core).
Axes of the slice: x: 2, y: 2, z: 4, core: 2. Of those that a mesh axis runs over, the one named last changes fastest.
Arguments:
- multipoles: bfloat16 [315, 2048], P(None, ('col', 'row')), may hold values from -6 to 6
- operators: bfloat16 [40, 315, 315], P('cores'), may hold values from -0.0078125 to 0.0078125
- classes: int32 [2048, 2048], P('row', 'col'), may hold values from 0 to 39, as said below
- separated: int32 [4, 4], P('row', 'col'), may hold values 0 or 1
- owners: int32 [2048], P('row'), may hold values from 0 to 7, as said below
Outputs:
- owned: float32 [315, 4096], P(None, ('row', 'col', 'cores'))
The draws below stay inside these ranges and needn't reach their ends.
Inputs may be any that keep to these rules, and one draw needn't show every extreme that they name: `owners`: in each block of 512 cells (cells b * 512 to b * 512 + 511) no owner holds more than 128 cells, and in every block one owner holds exactly 128. Cell t sits at (t % 8, (t // 8) % 4, t // 32) on a periodic grid of 8 x 4 x 2048 // 32 cells; classes[t, s] depends only on the wrapped offset between the positions of t and s.
All inputs are finite; a program needn't handle non-finite values. No bound on the sum of `separated` on one device may be relied on, other than what follows from the above.
Results may differ from the reference program's by a relative error of at most 0.0029.
Values may be sent and summed in bfloat16 or wider, within the bound.
A program may use at most 64 MiB of HBM per device.

```python
import jax
import jax.numpy as jnp
from jax import lax

P_SIZE = 315
TB = 512
NC = 2048
NK = 40
GROUP = 8
CAP = 128
N_ROW = 4


def draw_owners(key, part):

    def one_block(sub):
        first, second, third = jax.random.split(sub, 3)
        full = jax.random.randint(first, (), 0, GROUP)
        slot_owner = jnp.arange(2 * TB, dtype=jnp.int32) // CAP
        score = jax.random.permutation(second, 2 * TB).astype(jnp.int32)
        score = jnp.where(slot_owner == full, score - 4 * TB, score)
        order = jnp.argsort(score, stable=True)
        chosen = slot_owner[order[:TB]]
        return jax.random.permutation(third, chosen)
    keys = jax.random.split(jax.random.fold_in(key, 7), NC // TB)
    return jax.vmap(one_block)(keys).reshape(-1).astype(jnp.int32)


def draw_classes(key, part):
    depth = NC // 32
    table = jax.random.randint(jax.random.fold_in(key, 11), (8 * 4 * depth,), 0, NK).astype(jnp.int32)
    cells = jnp.arange(NC, dtype=jnp.int32)
    xpos = cells % 8
    ypos = cells // 8 % 4
    zpos = cells // 32
    dx = (xpos[:, None] - xpos[None, :]) % 8
    dy = (ypos[:, None] - ypos[None, :]) % 4
    dz = (zpos[:, None] - zpos[None, :]) % depth
    offset = (dz * 4 + dy) * 8 + dx
    return table[offset].astype(jnp.int32)


def touch_ends(drawn, rng, low, high):
    longest = drawn.shape.index(max(drawn.shape))
    spots = []
    for shift in (0, 1):
        where = [jax.random.randint(jax.random.fold_in(rng, axis), (), 0, length) for axis, length in enumerate(drawn.shape)]
        where[longest] = (where[longest] + shift) % drawn.shape[longest]
        spots.append(tuple(where))
    return drawn.at[spots[0]].set(low).at[spots[1]].set(high)


def block_levels(rng, shape, shards, smallest, high):
    gain, own = 1.0, jax.random.fold_in(rng, 6)
    for axis_at, parts in shards:
        steps = jnp.exp(jax.random.uniform(jax.random.fold_in(own, axis_at), (parts,), jnp.float32, smallest / len(shards), high / len(shards)))
        gain = gain * jnp.repeat(steps, shape[axis_at] // parts).reshape([-1 if axis == axis_at else 1 for axis in range(len(shape))])
    return gain


def bell_draw(stream_key, dims, scale, bound, cuts=(), kind=jnp.bfloat16):
    factor_of = block_levels(stream_key, dims, cuts, -0.22, 0.18) if cuts else 1.0
    result = jax.random.normal(stream_key, dims, jnp.float32) * scale * factor_of
    return jnp.minimum(jnp.maximum(result, -bound), bound).astype(kind)


def setup_inputs(seed: int = 0) -> dict:
    seeds = jax.random.split(jax.random.key(seed), 6)
    multipoles = bell_draw(seeds[0], (P_SIZE, NC), 1.0, 6.0, ((1, 16),))
    operators = bell_draw(seeds[1], (NK, P_SIZE, P_SIZE), (P_SIZE * NC) ** -0.5, 0.0078125, ((0, 2),))
    classes = draw_classes(jax.random.fold_in(seeds[5], 71), 0)
    separated = touch_ends((jax.random.randint(seeds[3], (N_ROW, N_ROW), 0, 4) < 3).astype(jnp.int32), jax.random.fold_in(seeds[3], 1), 0, 1)
    owners = draw_owners(jax.random.fold_in(seeds[5], 71), 0)
    return dict(multipoles=multipoles, operators=operators, classes=classes, separated=separated, owners=owners)


def reference(multipoles, operators, classes, separated, owners):
    cells = multipoles.shape[1]
    blocks = cells // TB
    block_of = jnp.arange(cells, dtype=jnp.int32) // TB
    weight = separated[block_of][:, block_of]

    def per_class(k, total):
        moved = jnp.dot(operators[k], multipoles, preferred_element_type=jnp.float32).astype(jnp.bfloat16)
        pick = jnp.where((classes == k) & (weight == 1), 1.0, 0.0).astype(jnp.float32)
        return total + jnp.dot(moved.astype(jnp.float32), pick.T, precision=lax.Precision.HIGHEST, preferred_element_type=jnp.float32)

    local = lax.fori_loop(0, operators.shape[0], per_class, jnp.zeros((multipoles.shape[0], cells), jnp.float32))
    owner_rows = owners.reshape(blocks, TB)
    hit = (owner_rows[:, None, :] == jnp.arange(GROUP, dtype=jnp.int32)[None, :, None]).astype(jnp.int32)
    before = jnp.cumsum(hit, axis=2) - hit
    rank = jnp.sum(before * hit, axis=1)
    target = ((jnp.arange(blocks, dtype=jnp.int32)[:, None] * GROUP + owner_rows) * CAP + rank).reshape(-1)
    owned = jnp.zeros((multipoles.shape[0], blocks * GROUP * CAP), jnp.float32).at[:, target].set(local)
    return owned
```

```python
import functools

import jax
import jax.numpy as jnp
from jax import lax
from jax.experimental import pallas as pl
from jax.experimental.pallas import tpu as pltpu
from jax.sharding import PartitionSpec as P

MESH = pl.DeviceIdType.MESH
F32 = jnp.float32
BF16 = jnp.bfloat16
CUTS = (128, 240)


def split_rows(rows):
    first = (rows // 2 + 15) // 16 * 16
    return ((0, first), (first, rows - first))


def kernel(
    dims,
    mult_hbm,
    op_hbm,
    cls_hbm,
    sep_ref,
    own_ref,
    out_ref,
    gath,
    mult,
    ops,
    cls,
    pick,
    moved,
    acc,
    place,
    psend0,
    psend1,
    precv0,
    precv1,
    zsend0,
    zsend1,
    zrecv0,
    zrecv1,
    local_sem,
    g_send,
    g_recv,
    p_send,
    p_recv,
    z_send,
    z_recv,
):
    n_row, n_col, n_core, spread = dims
    rows, width = mult_hbm.shape
    count = op_hbm.shape[0]
    targets, sources = cls_hbm.shape
    slots = zsend0.shape[2]
    group = n_col * n_core
    row = lax.axis_index("row")
    col = lax.axis_index("col")
    core = lax.axis_index("cores")
    parts = split_rows(rows)
    psend, precv = (psend0, psend1), (precv0, precv1)
    zsend, zrecv = (zsend0, zsend1), (zrecv0, zrecv1)

    barrier = pltpu.get_barrier_semaphore()
    for d in range(1, n_row):
        pl.semaphore_signal(
            barrier, inc=1, device_id={"row": lax.rem(row + d, n_row)}, device_id_type=MESH
        )
    for d in range(1, n_col):
        pl.semaphore_signal(
            barrier, inc=1, device_id={"col": lax.rem(col + d, n_col)}, device_id_type=MESH
        )
    pl.semaphore_signal(barrier, inc=1, device_id={"cores": 1 - core}, device_id_type=MESH)

    cls_copy = pltpu.make_async_copy(cls_hbm, cls, local_sem.at[0])
    cls_copy.start()
    own_copy = pltpu.make_async_copy(mult_hbm, gath.at[row], local_sem.at[1])
    own_copy.start()
    op_copy = pltpu.make_async_copy(op_hbm, ops, local_sem.at[2])
    op_copy.start()

    pl.semaphore_wait(barrier, n_row - 1 + n_col - 1 + 1)

    gathers = []
    for d in range(1, n_row):
        copy = pltpu.make_async_remote_copy(
            src_ref=mult_hbm,
            dst_ref=gath.at[row],
            send_sem=g_send.at[d - 1],
            recv_sem=g_recv.at[d - 1],
            device_id={"row": lax.rem(row + d, n_row)},
            device_id_type=MESH,
        )
        copy.start()
        gathers.append(copy)

    cls_copy.wait()
    per = sources // spread
    for j in range(spread):
        flag = sep_ref[0, j]
        block = cls[:, j * per : (j + 1) * per]
        wanted = (block - core * count) * flag + (flag - 1)
        turned = wanted.astype(F32).T
        for k in range(count):
            pick[pl.ds(k * sources + j * per, per), :] = jnp.where(
                turned == float(k), 1.0, 0.0
            ).astype(BF16)

    owners = own_ref[...]
    ids = lax.broadcasted_iota(jnp.int32, (group, targets), 0)
    hit = jnp.where(ids == owners, 1.0, 0.0)
    upper = jnp.where(
        lax.broadcasted_iota(jnp.int32, (targets, targets), 0)
        < lax.broadcasted_iota(jnp.int32, (targets, targets), 1),
        1.0,
        0.0,
    ).astype(BF16)
    before = jnp.dot(hit.astype(BF16), upper, preferred_element_type=F32)
    rank = jnp.sum(before * hit, axis=0, keepdims=True)
    slot = lax.broadcasted_iota(jnp.int32, (slots, targets), 0).astype(F32)
    for c in range(n_col):
        mine = jnp.where(owners == c * n_core + core, rank, -1.0)
        place[:, c * slots : (c + 1) * slots] = jnp.where(slot == mine, 1.0, 0.0).T.astype(BF16)

    own_copy.wait()
    for copy in gathers:
        copy.wait()
    if width % 128 == 0:
        for r in range(n_row):
            mult[:, r * width : (r + 1) * width] = gath[r]
    else:
        mult[...] = jnp.concatenate([gath[r] for r in range(n_row)], axis=1)
    op_copy.wait()

    def translate(part):
        start, size = parts[part]

        @pl.loop(0, count, unroll=4)
        def _(k):
            at = pl.multiple_of(k * sources, sources)
            moved[part * parts[0][1] : part * parts[0][1] + size, pl.ds(at, sources)] = jnp.dot(
                ops[k, start : start + size, :], mult[...], preferred_element_type=F32
            ).astype(BF16)

    def collect(part):
        start, size = parts[part]
        chunk = 10 if count % 10 == 0 else 1
        acc[0:size, :] = jnp.zeros((size, targets), F32)

        @pl.loop(0, count // chunk)
        def _(g):
            at = pl.multiple_of(g * chunk * sources, chunk * sources)
            acc[0:size, :] += jnp.dot(
                moved[part * parts[0][1] : part * parts[0][1] + size, pl.ds(at, chunk * sources)],
                pick[pl.ds(at, chunk * sources), :],
                preferred_element_type=F32,
            )

    def pair_start(part):
        size = parts[part][1]
        psend[part][...] = acc[0:size, :].astype(BF16)
        copy = pltpu.make_async_remote_copy(
            src_ref=psend[part],
            dst_ref=precv[part],
            send_sem=p_send.at[part],
            recv_sem=p_recv.at[part],
            device_id={"cores": 1 - core},
            device_id_type=MESH,
        )
        copy.start()
        return copy

    def spread_start(part, pair):
        size = parts[part][1]
        pair.wait()
        both = (psend[part][...].astype(F32) + precv[part][...].astype(F32)).astype(BF16)
        if slots % 128 == 0:
            placed = jnp.dot(both, place[...], preferred_element_type=F32).astype(BF16)
            for c in range(n_col):
                zsend[part][c] = placed[:, c * slots : (c + 1) * slots]
        else:
            for c in range(n_col):
                zsend[part][c] = jnp.dot(
                    both, place[:, c * slots : (c + 1) * slots], preferred_element_type=F32
                ).astype(BF16)
        copies = []
        for d in range(1, n_col):
            to = lax.rem(col + d, n_col)
            copy = pltpu.make_async_remote_copy(
                src_ref=zsend[part].at[to],
                dst_ref=zrecv[part].at[d - 1],
                send_sem=z_send.at[part, d - 1],
                recv_sem=z_recv.at[part, d - 1],
                device_id={"col": to},
                device_id_type=MESH,
            )
            copy.start()
            copies.append(copy)
        return copies

    def finish(part, copies):
        start, size = parts[part]
        for copy in copies:
            copy.wait()
        total = zsend[part][col].astype(F32)
        for d in range(1, n_col):
            total += zrecv[part][d - 1].astype(F32)
        out_ref[start : start + size, :] = total

    translate(0)
    collect(0)
    pair0 = pair_start(0)
    translate(1)
    sends0 = spread_start(0, pair0)
    collect(1)
    pair1 = pair_start(1)
    sends1 = spread_start(1, pair1)
    finish(0, sends0)
    finish(1, sends1)


def iota(shape, axis):
    return lax.broadcasted_iota(jnp.int32, shape, axis)


def mirror(spot, half, width, lead):
    upper = (spot >= half).astype(jnp.int32)
    within = spot - upper * half
    cell = (within >> 2) * 8 + upper * 4 + (within & 3) + lead * width
    return jnp.where(cell >= 2 * half, cell - 2 * half, cell)


def folded_kernel(
    dims,
    mult_hbm,
    op_hbm,
    cls_hbm,
    own_hbm,
    sep_ref,
    out_ref,
    gath,
    mult,
    ops,
    cls,
    own,
    pick,
    moved,
    place,
    psend,
    precv,
    zsend,
    zrecv,
    local_sem,
    g_send,
    g_recv,
    p_send,
    p_recv,
    z_send,
    z_recv,
):
    n_row, n_col, n_core, parts = dims
    rows, width = mult_hbm.shape
    count = op_hbm.shape[0]
    targets, sources = cls_hbm.shape
    slots = out_ref.shape[1]
    group = n_col * n_core
    half = sources // 2
    row = lax.axis_index("row")
    col = lax.axis_index("col")
    core = lax.axis_index("cores")

    barrier = pltpu.get_barrier_semaphore()
    for d in range(1, n_row):
        pl.semaphore_signal(
            barrier, inc=1, device_id={"row": lax.rem(row + d, n_row)}, device_id_type=MESH
        )
    pl.semaphore_signal(barrier, inc=1, device_id={"cores": 1 - core}, device_id_type=MESH)
    for d in range(1, n_col):
        pl.semaphore_signal(
            barrier, inc=1, device_id={"col": lax.rem(col + d, n_col)}, device_id_type=MESH
        )

    cls_copy = pltpu.make_async_copy(cls_hbm, cls, local_sem.at[0])
    own_copy = pltpu.make_async_copy(own_hbm, own, local_sem.at[1])
    mine_copy = pltpu.make_async_copy(mult_hbm, gath.at[row], local_sem.at[2])
    op_copy = pltpu.make_async_copy(op_hbm, ops, local_sem.at[3])
    for copy in (cls_copy, own_copy, mine_copy, op_copy):
        copy.start()

    pl.semaphore_wait(barrier, n_row - 1 + n_col - 1 + 1)

    def beside(dy, dx):
        return lax.rem(row // 2 + dy, 2) * 2 + lax.rem(lax.rem(row, 2) + dx, 2)

    gathers = []
    for d, (dy, dx) in enumerate(((0, 1), (1, 1), (1, 0))):
        copy = pltpu.make_async_remote_copy(
            src_ref=mult_hbm,
            dst_ref=gath.at[row],
            send_sem=g_send.at[d],
            recv_sem=g_recv.at[d],
            device_id={"row": beside(dy, dx)},
            device_id_type=MESH,
        )
        copy.start()
        gathers.append(copy)

    cls_copy.wait()
    step = 2 * width
    lead = row // 2
    square = (sources, sources)
    swap = jnp.where(
        mirror(iota(square, 0), half, step, 0) == iota(square, 1), 1.0, 0.0
    ).astype(BF16)
    turn = jnp.where(
        mirror(iota(square, 0), half, step, lead) == iota(square, 1), 1.0, 0.0
    ).astype(BF16)
    chosen = jnp.dot(
        swap[:half], cls[...].astype(F32).astype(BF16), preferred_element_type=F32
    ).astype(BF16)
    turned = lax.dot_general(
        turn, chosen, (((1,), (1,)), ((), ())), preferred_element_type=F32
    )
    flag = sep_ref[0, 0].astype(F32)
    wanted = ((turned - (core * count).astype(F32)) * flag + (flag - 1.0)).astype(BF16)
    one, zero = jnp.array(0.5, BF16), jnp.array(0.0, BF16)
    for k in range(count):
        same = jnp.where(wanted[0:half] == jnp.array(k, BF16), one, zero)
        other = jnp.where(wanted[half:] == jnp.array(k, BF16), one, zero)
        for which, both in enumerate((same + other, same - other)):
            for c in range(2):
                at = (c * count + k) * width
                pick[which, at : at + width, :] = both[c * width : (c + 1) * width]

    own_copy.wait()
    owners = own[...]
    ids = iota((group, targets), 0)
    hit = jnp.where(ids == owners, 1.0, 0.0)
    upper = jnp.where(
        iota((targets, targets), 0) < iota((targets, targets), 1), 1.0, 0.0
    ).astype(BF16)
    before = jnp.dot(hit.astype(BF16), upper, preferred_element_type=F32)
    rank = jnp.sum(before * hit, axis=0, keepdims=True)
    both = jnp.where(ids == 0, owners.astype(F32), rank).astype(BF16)
    both = lax.dot_general(both, swap, (((1,), (1,)), ((), ())), preferred_element_type=F32)
    owners, rank = both[0:1], both[1:2]
    slot = iota((slots, targets), 0).astype(F32)
    for c in range(n_col):
        wants = jnp.where(owners == (c * n_core + core).astype(F32), rank, -1.0)
        place[:, c * slots : (c + 1) * slots] = jnp.where(slot == wants, 1.0, 0.0).T.astype(BF16)

    order = jnp.where(
        mirror(iota((step, step), 1), width, step, 0) == iota((step, step), 0), 1.0, 0.0
    ).astype(BF16)

    def arrange(c):
        at = 2 * lax.rem(lead + c, 2)
        pair = jnp.concatenate([gath[at], gath[at + 1]], axis=1)
        mult[c] = jnp.dot(pair, order, preferred_element_type=F32).astype(BF16)

    def fold(got, start, size, c, k):
        low, high = got[:, :width], got[:, width:]
        at = (c * count + k) * width
        moved[0, start : start + size, at : at + width] = low + high
        moved[1, start : start + size, at : at + width] = low - high

    def translate(start, size, c):
        if size % 16 == 0:
            many = ops[:, start : start + size, :].reshape(count * size, rows)
            got = jnp.dot(many, mult[c], preferred_element_type=F32).astype(BF16)
            for k in range(count):
                fold(got[k * size : (k + 1) * size], start, size, c, k)
        else:
            for k in range(count):
                got = jnp.dot(
                    ops[k, start : start + size, :], mult[c], preferred_element_type=F32
                ).astype(BF16)
                fold(got, start, size, c, k)

    def collect(part):
        start, size = parts[part]
        size = (size + 15) // 16 * 16
        even = jnp.dot(moved[0, start : start + size], pick[0], preferred_element_type=F32)
        odd = jnp.dot(moved[1, start : start + size], pick[1], preferred_element_type=F32)
        psend[start : start + size, :half] = even + odd
        psend[start : start + size, half:] = even - odd
        copy = pltpu.make_async_remote_copy(
            src_ref=psend.at[pl.ds(start, size)],
            dst_ref=precv.at[pl.ds(start, size)],
            send_sem=p_send.at[part],
            recv_sem=p_recv.at[part],
            device_id={"cores": 1 - core},
            device_id_type=MESH,
        )
        copy.start()
        return copy

    def spread(part, pair):
        start, size = parts[part]
        size = (size + 15) // 16 * 16
        pair.wait()
        total = (psend[start : start + size] + precv[start : start + size]).astype(BF16)
        placed = jnp.dot(total, place[...], preferred_element_type=F32).astype(BF16)
        for c in range(n_col):
            zsend[c, start : start + size] = placed[:, c * slots : (c + 1) * slots]
        copies = []
        for d in range(1, n_col):
            to = lax.rem(col + d, n_col)
            copy = pltpu.make_async_remote_copy(
                src_ref=zsend.at[to, pl.ds(start, size)],
                dst_ref=zrecv.at[d - 1, pl.ds(start, size)],
                send_sem=z_send.at[part, d - 1],
                recv_sem=z_recv.at[part, d - 1],
                device_id={"col": to},
                device_id_type=MESH,
            )
            copy.start()
            copies.append(copy)
        return copies

    def finish(part, copies):
        start, size = parts[part]
        for copy in copies:
            copy.wait()
        total = zsend[col, start : start + size].astype(F32)
        for d in range(1, n_col):
            total += zrecv[d - 1, start : start + size].astype(F32)
        out_ref[start : start + size, :] = total

    mine_copy.wait()
    gathers[0].wait()
    arrange(0)
    op_copy.wait()
    translate(0, rows, 0)
    gathers[1].wait()
    gathers[2].wait()
    arrange(1)
    pairs, sends = [], []
    for part in range(len(parts)):
        translate(*parts[part], 1)
        if part > 0:
            sends.append(spread(part - 1, pairs[part - 1]))
        pairs.append(collect(part))
    sends.append(spread(len(parts) - 1, pairs[-1]))
    for part in range(len(parts)):
        finish(part, sends[part])


def folded(mesh, multipoles, operators, classes, separated, owners):
    n_row, n_col, n_core = mesh.shape["row"], mesh.shape["col"], mesh.shape["cores"]
    rows, width = multipoles.shape
    count = operators.shape[0]
    targets, sources = classes.shape
    slots = 2 * targets // (n_col * n_core)
    cuts = [0, *CUTS, rows]
    parts = tuple((at, to - at) for at, to in zip(cuts, cuts[1:]))
    n, top = len(parts), (rows + 15) // 16 * 16
    hbm = pl.BlockSpec(memory_space=pltpu.HBM)
    dma = pltpu.SemaphoreType.DMA
    operands = [
        pltpu.with_memory_space_constraint(x, pltpu.HBM)
        for x in (multipoles, operators, classes, owners.reshape(1, targets))
    ]
    return pl.pallas_call(
        functools.partial(folded_kernel, (n_row, n_col, n_core, parts)),
        out_shape=jax.ShapeDtypeStruct((rows, slots), F32),
        in_specs=[hbm] * 4 + [pl.BlockSpec(memory_space=pltpu.SMEM)],
        out_specs=pl.BlockSpec(memory_space=pltpu.VMEM),
        scratch_shapes=[
            pltpu.VMEM((n_row, rows, width), BF16),
            pltpu.VMEM((2, rows, 2 * width), BF16),
            pltpu.VMEM((count, rows, rows), BF16),
            pltpu.VMEM((targets, sources), jnp.int32),
            pltpu.VMEM((1, targets), jnp.int32),
            pltpu.VMEM((2, count * sources // 2, targets // 2), BF16),
            pltpu.VMEM((2, top, count * sources // 2), BF16),
            pltpu.VMEM((targets, n_col * slots), BF16),
            pltpu.VMEM((top, targets), F32),
            pltpu.VMEM((top, targets), F32),
            pltpu.VMEM((n_col, top, slots), BF16),
            pltpu.VMEM((n_col - 1, top, slots), BF16),
            dma((4,)),
            dma((n_row - 1,)),
            dma((n_row - 1,)),
            dma((n,)),
            dma((n,)),
            dma((n, n_col - 1)),
            dma((n, n_col - 1)),
        ],
        compiler_params=pltpu.CompilerParams(
            collective_id=0, has_side_effects=True, vmem_limit_bytes=44 * 1024 * 1024
        ),
    )(*operands, separated)


def solution(mesh):
    n_row, n_col, n_core = mesh.shape["row"], mesh.shape["col"], mesh.shape["cores"]

    def shards(multipoles, operators, classes, separated, owners):
        rows, width = multipoles.shape
        count = operators.shape[0]
        targets, sources = classes.shape
        slots = 2 * targets // (n_col * n_core)
        if separated.shape[1] == 1 and n_row == 4 and n_core == 2 and width % 128 == 0:
            return folded(mesh, multipoles, operators, classes, separated, owners)
        sizes = [size for _, size in split_rows(rows)]
        top = sizes[0] * 2
        hbm = pl.BlockSpec(memory_space=pl.ANY)
        dma = pltpu.SemaphoreType.DMA
        return pl.pallas_call(
            functools.partial(kernel, (n_row, n_col, n_core, separated.shape[1])),
            out_shape=jax.ShapeDtypeStruct((rows, slots), F32),
            in_specs=[
                hbm,
                hbm,
                hbm,
                pl.BlockSpec(memory_space=pltpu.SMEM),
                pl.BlockSpec(memory_space=pltpu.VMEM),
            ],
            out_specs=pl.BlockSpec(memory_space=pltpu.VMEM),
            scratch_shapes=[
                pltpu.VMEM((n_row, rows, width), BF16),
                pltpu.VMEM((rows, sources), BF16),
                pltpu.VMEM((count, rows, rows), BF16),
                pltpu.VMEM((targets, sources), jnp.int32),
                pltpu.VMEM((count * sources, targets), BF16),
                pltpu.VMEM((top, count * sources), BF16),
                pltpu.VMEM((sizes[0], targets), F32),
                pltpu.VMEM((targets, n_col * slots), BF16),
            ]
            + [pltpu.VMEM((size, targets), BF16) for size in sizes]
            + [pltpu.VMEM((size, targets), BF16) for size in sizes]
            + [pltpu.VMEM((n_col, size, slots), BF16) for size in sizes]
            + [pltpu.VMEM((n_col - 1, size, slots), BF16) for size in sizes]
            + [
                dma((3,)),
                dma((n_row - 1,)),
                dma((n_row - 1,)),
                dma((2,)),
                dma((2,)),
                dma((2, n_col - 1)),
                dma((2, n_col - 1)),
            ],
            compiler_params=pltpu.CompilerParams(
                collective_id=0, has_side_effects=True, vmem_limit_bytes=60 * 1024 * 1024
            ),
        )(multipoles, operators, classes, separated, owners.reshape(1, targets))

    return jax.shard_map(
        shards,
        mesh=mesh,
        in_specs=(
            P(None, ("col", "row")),
            P("cores", None, None),
            P("row", "col"),
            P("row", "col"),
            P("row"),
        ),
        out_specs=P(None, ("row", "col", "cores")),
        check_vma=False,
    )
```

```python
import functools

import jax
import jax.numpy as jnp
from jax import lax
from jax.experimental import pallas as pl
from jax.experimental.pallas import tpu as pltpu
from jax.sharding import PartitionSpec as P

MESH = pl.DeviceIdType.MESH
F32 = jnp.float32
BF16 = jnp.bfloat16
CUTS = (96, 208)


def split_rows(rows):
    first = (rows // 2 + 15) // 16 * 16
    return ((0, first), (first, rows - first))


def kernel(
    dims,
    mult_hbm,
    op_hbm,
    cls_hbm,
    sep_ref,
    own_ref,
    out_ref,
    gath,
    mult,
    ops,
    cls,
    pick,
    moved,
    acc,
    place,
    psend0,
    psend1,
    precv0,
    precv1,
    zsend0,
    zsend1,
    zrecv0,
    zrecv1,
    local_sem,
    g_send,
    g_recv,
    p_send,
    p_recv,
    z_send,
    z_recv,
):
    n_row, n_col, n_core, spread = dims
    rows, width = mult_hbm.shape
    count = op_hbm.shape[0]
    targets, sources = cls_hbm.shape
    slots = zsend0.shape[2]
    group = n_col * n_core
    row = lax.axis_index("row")
    col = lax.axis_index("col")
    core = lax.axis_index("cores")
    parts = split_rows(rows)
    psend, precv = (psend0, psend1), (precv0, precv1)
    zsend, zrecv = (zsend0, zsend1), (zrecv0, zrecv1)

    barrier = pltpu.get_barrier_semaphore()
    for d in range(1, n_row):
        pl.semaphore_signal(
            barrier, inc=1, device_id={"row": lax.rem(row + d, n_row)}, device_id_type=MESH
        )
    for d in range(1, n_col):
        pl.semaphore_signal(
            barrier, inc=1, device_id={"col": lax.rem(col + d, n_col)}, device_id_type=MESH
        )
    pl.semaphore_signal(barrier, inc=1, device_id={"cores": 1 - core}, device_id_type=MESH)

    cls_copy = pltpu.make_async_copy(cls_hbm, cls, local_sem.at[0])
    cls_copy.start()
    own_copy = pltpu.make_async_copy(mult_hbm, gath.at[row], local_sem.at[1])
    own_copy.start()
    op_copy = pltpu.make_async_copy(op_hbm, ops, local_sem.at[2])
    op_copy.start()

    pl.semaphore_wait(barrier, n_row - 1 + n_col - 1 + 1)

    gathers = []
    for d in range(1, n_row):
        copy = pltpu.make_async_remote_copy(
            src_ref=mult_hbm,
            dst_ref=gath.at[row],
            send_sem=g_send.at[d - 1],
            recv_sem=g_recv.at[d - 1],
            device_id={"row": lax.rem(row + d, n_row)},
            device_id_type=MESH,
        )
        copy.start()
        gathers.append(copy)

    cls_copy.wait()
    per = sources // spread
    for j in range(spread):
        flag = sep_ref[0, j]
        block = cls[:, j * per : (j + 1) * per]
        wanted = (block - core * count) * flag + (flag - 1)
        turned = wanted.astype(F32).T
        for k in range(count):
            pick[pl.ds(k * sources + j * per, per), :] = jnp.where(
                turned == float(k), 1.0, 0.0
            ).astype(BF16)

    owners = own_ref[...]
    ids = lax.broadcasted_iota(jnp.int32, (group, targets), 0)
    hit = jnp.where(ids == owners, 1.0, 0.0)
    upper = jnp.where(
        lax.broadcasted_iota(jnp.int32, (targets, targets), 0)
        < lax.broadcasted_iota(jnp.int32, (targets, targets), 1),
        1.0,
        0.0,
    ).astype(BF16)
    before = jnp.dot(hit.astype(BF16), upper, preferred_element_type=F32)
    rank = jnp.sum(before * hit, axis=0, keepdims=True)
    slot = lax.broadcasted_iota(jnp.int32, (slots, targets), 0).astype(F32)
    for c in range(n_col):
        mine = jnp.where(owners == c * n_core + core, rank, -1.0)
        place[:, c * slots : (c + 1) * slots] = jnp.where(slot == mine, 1.0, 0.0).T.astype(BF16)

    own_copy.wait()
    for copy in gathers:
        copy.wait()
    if width % 128 == 0:
        for r in range(n_row):
            mult[:, r * width : (r + 1) * width] = gath[r]
    else:
        mult[...] = jnp.concatenate([gath[r] for r in range(n_row)], axis=1)
    op_copy.wait()

    def translate(part):
        start, size = parts[part]

        @pl.loop(0, count, unroll=4)
        def _(k):
            at = pl.multiple_of(k * sources, sources)
            moved[part * parts[0][1] : part * parts[0][1] + size, pl.ds(at, sources)] = jnp.dot(
                ops[k, start : start + size, :], mult[...], preferred_element_type=F32
            ).astype(BF16)

    def collect(part):
        start, size = parts[part]
        chunk = 10 if count % 10 == 0 else 1
        acc[0:size, :] = jnp.zeros((size, targets), F32)

        @pl.loop(0, count // chunk)
        def _(g):
            at = pl.multiple_of(g * chunk * sources, chunk * sources)
            acc[0:size, :] += jnp.dot(
                moved[part * parts[0][1] : part * parts[0][1] + size, pl.ds(at, chunk * sources)],
                pick[pl.ds(at, chunk * sources), :],
                preferred_element_type=F32,
            )

    def pair_start(part):
        size = parts[part][1]
        psend[part][...] = acc[0:size, :].astype(BF16)
        copy = pltpu.make_async_remote_copy(
            src_ref=psend[part],
            dst_ref=precv[part],
            send_sem=p_send.at[part],
            recv_sem=p_recv.at[part],
            device_id={"cores": 1 - core},
            device_id_type=MESH,
        )
        copy.start()
        return copy

    def spread_start(part, pair):
        size = parts[part][1]
        pair.wait()
        both = (psend[part][...].astype(F32) + precv[part][...].astype(F32)).astype(BF16)
        if slots % 128 == 0:
            placed = jnp.dot(both, place[...], preferred_element_type=F32).astype(BF16)
            for c in range(n_col):
                zsend[part][c] = placed[:, c * slots : (c + 1) * slots]
        else:
            for c in range(n_col):
                zsend[part][c] = jnp.dot(
                    both, place[:, c * slots : (c + 1) * slots], preferred_element_type=F32
                ).astype(BF16)
        copies = []
        for d in range(1, n_col):
            to = lax.rem(col + d, n_col)
            copy = pltpu.make_async_remote_copy(
                src_ref=zsend[part].at[to],
                dst_ref=zrecv[part].at[d - 1],
                send_sem=z_send.at[part, d - 1],
                recv_sem=z_recv.at[part, d - 1],
                device_id={"col": to},
                device_id_type=MESH,
            )
            copy.start()
            copies.append(copy)
        return copies

    def finish(part, copies):
        start, size = parts[part]
        for copy in copies:
            copy.wait()
        total = zsend[part][col].astype(F32)
        for d in range(1, n_col):
            total += zrecv[part][d - 1].astype(F32)
        out_ref[start : start + size, :] = total

    translate(0)
    collect(0)
    pair0 = pair_start(0)
    translate(1)
    sends0 = spread_start(0, pair0)
    collect(1)
    pair1 = pair_start(1)
    sends1 = spread_start(1, pair1)
    finish(0, sends0)
    finish(1, sends1)


def iota(shape, axis):
    return lax.broadcasted_iota(jnp.int32, shape, axis)


def mirror(spot, half):
    upper = (spot >= half).astype(jnp.int32)
    within = spot - upper * half
    return (within >> 2) * 8 + upper * 4 + (within & 3)


def folded_kernel(
    dims,
    mult_hbm,
    op_hbm,
    cls_hbm,
    own_hbm,
    sep_ref,
    out_ref,
    gath,
    mult,
    ops,
    cls,
    own,
    pick,
    moved,
    place,
    acc,
    psend,
    precv,
    zsend,
    zrecv,
    local_sem,
    g_send,
    g_recv,
    p_send,
    p_recv,
    z_send,
    z_recv,
):
    n_row, n_col, n_core, parts = dims
    rows, width = mult_hbm.shape
    count = op_hbm.shape[0]
    targets, sources = cls_hbm.shape
    slots = out_ref.shape[1]
    group = n_col * n_core
    half = sources // 2
    row = lax.axis_index("row")
    col = lax.axis_index("col")
    core = lax.axis_index("cores")

    barrier = pltpu.get_barrier_semaphore()
    for d in range(1, n_row):
        pl.semaphore_signal(
            barrier, inc=1, device_id={"row": lax.rem(row + d, n_row)}, device_id_type=MESH
        )
    pl.semaphore_signal(barrier, inc=1, device_id={"cores": 1 - core}, device_id_type=MESH)
    for d in range(1, n_col):
        pl.semaphore_signal(
            barrier, inc=1, device_id={"col": lax.rem(col + d, n_col)}, device_id_type=MESH
        )

    cls_copy = pltpu.make_async_copy(cls_hbm, cls, local_sem.at[0])
    own_copy = pltpu.make_async_copy(own_hbm, own, local_sem.at[1])
    mine_copy = pltpu.make_async_copy(mult_hbm, gath.at[row], local_sem.at[2])
    op_copy = pltpu.make_async_copy(op_hbm, ops, local_sem.at[3])
    for copy in (cls_copy, own_copy, mine_copy, op_copy):
        copy.start()

    pl.semaphore_wait(barrier, n_row - 1 + n_col - 1 + 1)

    def beside(dy, dx):
        return lax.rem(row // 2 + dy, 2) * 2 + lax.rem(lax.rem(row, 2) + dx, 2)

    gathers = []
    for d, (dy, dx) in enumerate(((0, 1), (1, 1), (1, 0))):
        copy = pltpu.make_async_remote_copy(
            src_ref=mult_hbm,
            dst_ref=gath.at[row],
            send_sem=g_send.at[d],
            recv_sem=g_recv.at[d],
            device_id={"row": beside(dy, dx)},
            device_id_type=MESH,
        )
        copy.start()
        gathers.append(copy)

    cls_copy.wait()
    step = 2 * width
    lead = row // 2
    square = (sources, sources)
    swap = jnp.where(
        mirror(iota(square, 0), half) == iota(square, 1), 1.0, 0.0
    ).astype(BF16)
    spot = iota(square, 0)
    upper = (spot >= half).astype(jnp.int32)
    spot = spot - upper * half
    small = width // 2
    spot, base = (
        jnp.where(
            spot < small, spot, jnp.where(spot < width, spot - small, spot - width)
        ),
        jnp.where(
            spot < small,
            row * width,
            jnp.where(spot < width, beside(0, 1) * width, lax.rem(lead + 1, 2) * step),
        ),
    )
    turn = jnp.where(
        base + (spot >> 2) * 8 + upper * 4 + (spot & 3) == iota(square, 1), 1.0, 0.0
    ).astype(BF16)
    chosen = jnp.dot(
        swap[:half], cls[...].astype(F32).astype(BF16), preferred_element_type=F32
    ).astype(BF16)
    turned = lax.dot_general(
        turn, chosen, (((1,), (1,)), ((), ())), preferred_element_type=F32
    )
    flag = sep_ref[0, 0].astype(F32)
    wanted = ((turned - (core * count).astype(F32)) * flag + (flag - 1.0)).astype(BF16)
    chunks = (
        (0, 0, small),
        (count * small, small, small),
        (count * width, width, width),
    )
    one, zero = jnp.array(0.5, BF16), jnp.array(0.0, BF16)
    @pl.loop(0, count, unroll=4)
    def _(k):
        kind = jnp.asarray(k, F32).astype(BF16)
        same = jnp.where(wanted[0:half] == kind, one, zero)
        other = jnp.where(wanted[half:] == kind, one, zero)
        for which, both in enumerate((same + other, same - other)):
            for at, first, size in chunks:
                to = pl.multiple_of(at + k * size, size)
                pick[which, pl.ds(to, size), :] = both[first : first + size]

    own_copy.wait()
    owners = own[...]
    ids = iota((group, targets), 0)
    hit = jnp.where(ids == owners, 1.0, 0.0)
    upper = jnp.where(
        iota((targets, targets), 0) < iota((targets, targets), 1), 1.0, 0.0
    ).astype(BF16)
    before = jnp.dot(hit.astype(BF16), upper, preferred_element_type=F32)
    rank = jnp.sum(before * hit, axis=0, keepdims=True)
    both = jnp.where(ids == 0, owners.astype(F32), rank).astype(BF16)
    both = lax.dot_general(both, swap, (((1,), (1,)), ((), ())), preferred_element_type=F32)
    owners, rank = both[0:1], both[1:2]
    slot = iota((slots, targets), 0).astype(F32)
    for c in range(n_col):
        wants = jnp.where(owners == (c * n_core + core).astype(F32), rank, -1.0)
        place[:, c * slots : (c + 1) * slots] = jnp.where(slot == wants, 1.0, 0.0).T.astype(BF16)

    def arrange(at, many):
        wide = many * width
        order = jnp.where(
            mirror(iota((wide, wide), 1), wide // 2) == iota((wide, wide), 0), 1.0, 0.0
        ).astype(BF16)
        cells = [gath[at + i] for i in range(many)]
        cells = cells[0] if many == 1 else jnp.concatenate(cells, axis=1)
        return jnp.dot(cells, order, preferred_element_type=F32).astype(BF16)

    left = iota((1, width), 1) < small

    def translate_one(which, cells):
        for k in range(0, count, 2):
            got = [
                jnp.dot(ops[k + i], cells, preferred_element_type=F32).astype(BF16)
                for i in range(2)
            ]
            back = [pltpu.roll(g.astype(F32), small, 1).astype(BF16) for g in got]
            at = (which * count + k) * small
            moved[0, 0:rows, at : at + width] = jnp.where(
                left, got[0] + back[0], got[1] + back[1]
            )
            moved[1, 0:rows, at : at + width] = jnp.where(
                left, got[0] - back[0], back[1] - got[1]
            )

    def fold(got, start, size, c, k):
        low, high = got[:, :width], got[:, width:]
        at = (c * count + k) * width
        moved[0, start : start + size, at : at + width] = low + high
        moved[1, start : start + size, at : at + width] = low - high

    def translate(start, size):
        c = 1
        if size % 16 == 0:
            many = ops[:, start : start + size, :].reshape(count * size, rows)
            got = jnp.dot(many, mult[...], preferred_element_type=F32).astype(BF16)
            for k in range(count):
                fold(got[k * size : (k + 1) * size], start, size, c, k)
        else:
            for k in range(count):
                got = jnp.dot(
                    ops[k, start : start + size, :], mult[...], preferred_element_type=F32
                ).astype(BF16)
                fold(got, start, size, c, k)

    def collect(part):
        start, size = parts[part]
        size = (size + 15) // 16 * 16
        begin = count * small
        for which in range(2):
            acc[which, start : start + size] += jnp.dot(
                moved[which, start : start + size, begin:],
                pick[which, begin:, :],
                preferred_element_type=F32,
            )
        even, odd = acc[0, start : start + size], acc[1, start : start + size]
        psend[start : start + size, :half] = even + odd
        psend[start : start + size, half:] = even - odd
        copy = pltpu.make_async_remote_copy(
            src_ref=psend.at[pl.ds(start, size)],
            dst_ref=precv.at[pl.ds(start, size)],
            send_sem=p_send.at[part],
            recv_sem=p_recv.at[part],
            device_id={"cores": 1 - core},
            device_id_type=MESH,
        )
        copy.start()
        return copy

    def spread(part, pair):
        start, size = parts[part]
        size = (size + 15) // 16 * 16
        pair.wait()
        total = (psend[start : start + size] + precv[start : start + size]).astype(BF16)
        placed = jnp.dot(total, place[...], preferred_element_type=F32).astype(BF16)
        for c in range(n_col):
            zsend[c, start : start + size] = placed[:, c * slots : (c + 1) * slots]
        copies = []
        for d in range(1, n_col):
            to = lax.rem(col + d, n_col)
            copy = pltpu.make_async_remote_copy(
                src_ref=zsend.at[to, pl.ds(start, size)],
                dst_ref=zrecv.at[d - 1, pl.ds(start, size)],
                send_sem=z_send.at[part, d - 1],
                recv_sem=z_recv.at[part, d - 1],
                device_id={"col": to},
                device_id_type=MESH,
            )
            copy.start()
            copies.append(copy)
        return copies

    def finish(part, copies):
        start, size = parts[part]
        for copy in copies:
            copy.wait()
        total = zsend[col, start : start + size].astype(F32)
        for d in range(1, n_col):
            total += zrecv[d - 1, start : start + size].astype(F32)
        out_ref[start : start + size, :] = total

    mine_copy.wait()
    cells = arrange(row, 1)
    op_copy.wait()
    translate_one(0, cells)
    for which in range(2):
        acc[which] = jnp.dot(
            moved[which, :, : count * small],
            pick[which, : count * small, :],
            preferred_element_type=F32,
        )
    gathers[0].wait()
    translate_one(1, arrange(beside(0, 1), 1))
    gathers[1].wait()
    gathers[2].wait()
    mult[...] = arrange(2 * lax.rem(lead + 1, 2), 2)
    pairs, sends = [], []
    for part in range(len(parts)):
        translate(*parts[part])
        if part > 0:
            sends.append(spread(part - 1, pairs[part - 1]))
        pairs.append(collect(part))
    sends.append(spread(len(parts) - 1, pairs[-1]))
    for part in range(len(parts)):
        finish(part, sends[part])


def folded(mesh, multipoles, operators, classes, separated, owners):
    n_row, n_col, n_core = mesh.shape["row"], mesh.shape["col"], mesh.shape["cores"]
    rows, width = multipoles.shape
    count = operators.shape[0]
    targets, sources = classes.shape
    slots = 2 * targets // (n_col * n_core)
    cuts = [0, *CUTS, rows]
    parts = tuple((at, to - at) for at, to in zip(cuts, cuts[1:]))
    n, top = len(parts), (rows + 15) // 16 * 16
    hbm = pl.BlockSpec(memory_space=pltpu.HBM)
    dma = pltpu.SemaphoreType.DMA
    operands = [
        pltpu.with_memory_space_constraint(x, pltpu.HBM)
        for x in (multipoles, operators, classes, owners.reshape(1, targets))
    ]
    return pl.pallas_call(
        functools.partial(folded_kernel, (n_row, n_col, n_core, parts)),
        out_shape=jax.ShapeDtypeStruct((rows, slots), F32),
        in_specs=[hbm] * 4 + [pl.BlockSpec(memory_space=pltpu.SMEM)],
        out_specs=pl.BlockSpec(memory_space=pltpu.VMEM),
        scratch_shapes=[
            pltpu.VMEM((n_row, rows, width), BF16),
            pltpu.VMEM((rows, 2 * width), BF16),
            pltpu.VMEM((count, rows, rows), BF16),
            pltpu.VMEM((targets, sources), jnp.int32),
            pltpu.VMEM((1, targets), jnp.int32),
            pltpu.VMEM((2, count * sources // 2, targets // 2), BF16),
            pltpu.VMEM((2, top, count * sources // 2), BF16),
            pltpu.VMEM((targets, n_col * slots), BF16),
            pltpu.VMEM((2, top, targets // 2), F32),
            pltpu.VMEM((top, targets), F32),
            pltpu.VMEM((top, targets), F32),
            pltpu.VMEM((n_col, top, slots), BF16),
            pltpu.VMEM((n_col - 1, top, slots), BF16),
            dma((4,)),
            dma((n_row - 1,)),
            dma((n_row - 1,)),
            dma((n,)),
            dma((n,)),
            dma((n, n_col - 1)),
            dma((n, n_col - 1)),
        ],
        compiler_params=pltpu.CompilerParams(
            collective_id=0, has_side_effects=True, vmem_limit_bytes=44 * 1024 * 1024
        ),
    )(*operands, separated)


def solution(mesh):
    n_row, n_col, n_core = mesh.shape["row"], mesh.shape["col"], mesh.shape["cores"]

    def shards(multipoles, operators, classes, separated, owners):
        rows, width = multipoles.shape
        count = operators.shape[0]
        targets, sources = classes.shape
        slots = 2 * targets // (n_col * n_core)
        if separated.shape[1] == 1 and n_row == 4 and n_core == 2 and width % 128 == 0:
            return folded(mesh, multipoles, operators, classes, separated, owners)
        sizes = [size for _, size in split_rows(rows)]
        top = sizes[0] * 2
        hbm = pl.BlockSpec(memory_space=pl.ANY)
        dma = pltpu.SemaphoreType.DMA
        return pl.pallas_call(
            functools.partial(kernel, (n_row, n_col, n_core, separated.shape[1])),
            out_shape=jax.ShapeDtypeStruct((rows, slots), F32),
            in_specs=[
                hbm,
                hbm,
                hbm,
                pl.BlockSpec(memory_space=pltpu.SMEM),
                pl.BlockSpec(memory_space=pltpu.VMEM),
            ],
            out_specs=pl.BlockSpec(memory_space=pltpu.VMEM),
            scratch_shapes=[
                pltpu.VMEM((n_row, rows, width), BF16),
                pltpu.VMEM((rows, sources), BF16),
                pltpu.VMEM((count, rows, rows), BF16),
                pltpu.VMEM((targets, sources), jnp.int32),
                pltpu.VMEM((count * sources, targets), BF16),
                pltpu.VMEM((top, count * sources), BF16),
                pltpu.VMEM((sizes[0], targets), F32),
                pltpu.VMEM((targets, n_col * slots), BF16),
            ]
            + [pltpu.VMEM((size, targets), BF16) for size in sizes]
            + [pltpu.VMEM((size, targets), BF16) for size in sizes]
            + [pltpu.VMEM((n_col, size, slots), BF16) for size in sizes]
            + [pltpu.VMEM((n_col - 1, size, slots), BF16) for size in sizes]
            + [
                dma((3,)),
                dma((n_row - 1,)),
                dma((n_row - 1,)),
                dma((2,)),
                dma((2,)),
                dma((2, n_col - 1)),
                dma((2, n_col - 1)),
            ],
            compiler_params=pltpu.CompilerParams(
                collective_id=0, has_side_effects=True, vmem_limit_bytes=60 * 1024 * 1024
            ),
        )(multipoles, operators, classes, separated, owners.reshape(1, targets))

    return jax.shard_map(
        shards,
        mesh=mesh,
        in_specs=(
            P(None, ("col", "row")),
            P("cores", None, None),
            P("row", "col"),
            P("row", "col"),
            P("row"),
        ),
        out_specs=P(None, ("row", "col", "cores")),
        check_vma=False,
    )
```

```python
import functools

import jax
import jax.numpy as jnp
from jax import lax
from jax.experimental import pallas as pl
from jax.experimental.pallas import tpu as pltpu
from jax.sharding import PartitionSpec as P

MESH = pl.DeviceIdType.MESH
F32 = jnp.float32
BF16 = jnp.bfloat16
CUTS = (96, 208)


def split_rows(rows):
    first = (rows // 2 + 15) // 16 * 16
    return ((0, first), (first, rows - first))


def kernel(
    dims,
    mult_hbm,
    op_hbm,
    cls_hbm,
    sep_ref,
    own_ref,
    out_ref,
    gath,
    mult,
    ops,
    cls,
    pick,
    moved,
    acc,
    place,
    psend0,
    psend1,
    precv0,
    precv1,
    zsend0,
    zsend1,
    zrecv0,
    zrecv1,
    local_sem,
    g_send,
    g_recv,
    p_send,
    p_recv,
    z_send,
    z_recv,
):
    n_row, n_col, n_core, spread = dims
    rows, width = mult_hbm.shape
    count = op_hbm.shape[0]
    targets, sources = cls_hbm.shape
    slots = zsend0.shape[2]
    group = n_col * n_core
    row = lax.axis_index("row")
    col = lax.axis_index("col")
    core = lax.axis_index("cores")
    parts = split_rows(rows)
    psend, precv = (psend0, psend1), (precv0, precv1)
    zsend, zrecv = (zsend0, zsend1), (zrecv0, zrecv1)

    barrier = pltpu.get_barrier_semaphore()
    for d in range(1, n_row):
        pl.semaphore_signal(
            barrier, inc=1, device_id={"row": lax.rem(row + d, n_row)}, device_id_type=MESH
        )
    for d in range(1, n_col):
        pl.semaphore_signal(
            barrier, inc=1, device_id={"col": lax.rem(col + d, n_col)}, device_id_type=MESH
        )
    pl.semaphore_signal(barrier, inc=1, device_id={"cores": 1 - core}, device_id_type=MESH)

    cls_copy = pltpu.make_async_copy(cls_hbm, cls, local_sem.at[0])
    cls_copy.start()
    own_copy = pltpu.make_async_copy(mult_hbm, gath.at[row], local_sem.at[1])
    own_copy.start()
    op_copy = pltpu.make_async_copy(op_hbm, ops, local_sem.at[2])
    op_copy.start()

    pl.semaphore_wait(barrier, n_row - 1 + n_col - 1 + 1)

    gathers = []
    for d in range(1, n_row):
        copy = pltpu.make_async_remote_copy(
            src_ref=mult_hbm,
            dst_ref=gath.at[row],
            send_sem=g_send.at[d - 1],
            recv_sem=g_recv.at[d - 1],
            device_id={"row": lax.rem(row + d, n_row)},
            device_id_type=MESH,
        )
        copy.start()
        gathers.append(copy)

    cls_copy.wait()
    per = sources // spread
    for j in range(spread):
        flag = sep_ref[0, j]
        block = cls[:, j * per : (j + 1) * per]
        wanted = (block - core * count) * flag + (flag - 1)
        turned = wanted.astype(F32).T
        for k in range(count):
            pick[pl.ds(k * sources + j * per, per), :] = jnp.where(
                turned == float(k), 1.0, 0.0
            ).astype(BF16)

    owners = own_ref[...]
    ids = lax.broadcasted_iota(jnp.int32, (group, targets), 0)
    hit = jnp.where(ids == owners, 1.0, 0.0)
    upper = jnp.where(
        lax.broadcasted_iota(jnp.int32, (targets, targets), 0)
        < lax.broadcasted_iota(jnp.int32, (targets, targets), 1),
        1.0,
        0.0,
    ).astype(BF16)
    before = jnp.dot(hit.astype(BF16), upper, preferred_element_type=F32)
    rank = jnp.sum(before * hit, axis=0, keepdims=True)
    slot = lax.broadcasted_iota(jnp.int32, (slots, targets), 0).astype(F32)
    for c in range(n_col):
        mine = jnp.where(owners == c * n_core + core, rank, -1.0)
        place[:, c * slots : (c + 1) * slots] = jnp.where(slot == mine, 1.0, 0.0).T.astype(BF16)

    own_copy.wait()
    for copy in gathers:
        copy.wait()
    if width % 128 == 0:
        for r in range(n_row):
            mult[:, r * width : (r + 1) * width] = gath[r]
    else:
        mult[...] = jnp.concatenate([gath[r] for r in range(n_row)], axis=1)
    op_copy.wait()

    def translate(part):
        start, size = parts[part]

        @pl.loop(0, count, unroll=10)
        def _(k):
            at = pl.multiple_of(k * sources, sources)
            moved[part * parts[0][1] : part * parts[0][1] + size, pl.ds(at, sources)] = jnp.dot(
                ops[k, start : start + size, :], mult[...], preferred_element_type=F32
            ).astype(BF16)

    def collect(part):
        start, size = parts[part]
        chunk = 10 if count % 10 == 0 else 1
        acc[0:size, :] = jnp.zeros((size, targets), F32)

        @pl.loop(0, count // chunk)
        def _(g):
            at = pl.multiple_of(g * chunk * sources, chunk * sources)
            acc[0:size, :] += jnp.dot(
                moved[part * parts[0][1] : part * parts[0][1] + size, pl.ds(at, chunk * sources)],
                pick[pl.ds(at, chunk * sources), :],
                preferred_element_type=F32,
            )

    def pair_start(part):
        size = parts[part][1]
        psend[part][...] = acc[0:size, :].astype(BF16)
        copy = pltpu.make_async_remote_copy(
            src_ref=psend[part],
            dst_ref=precv[part],
            send_sem=p_send.at[part],
            recv_sem=p_recv.at[part],
            device_id={"cores": 1 - core},
            device_id_type=MESH,
        )
        copy.start()
        return copy

    def spread_start(part, pair):
        size = parts[part][1]
        pair.wait()
        both = (psend[part][...].astype(F32) + precv[part][...].astype(F32)).astype(BF16)
        if slots % 128 == 0:
            placed = jnp.dot(both, place[...], preferred_element_type=F32).astype(BF16)
            for c in range(n_col):
                zsend[part][c] = placed[:, c * slots : (c + 1) * slots]
        else:
            for c in range(n_col):
                zsend[part][c] = jnp.dot(
                    both, place[:, c * slots : (c + 1) * slots], preferred_element_type=F32
                ).astype(BF16)
        copies = []
        for d in range(1, n_col):
            to = lax.rem(col + d, n_col)
            copy = pltpu.make_async_remote_copy(
                src_ref=zsend[part].at[to],
                dst_ref=zrecv[part].at[d - 1],
                send_sem=z_send.at[part, d - 1],
                recv_sem=z_recv.at[part, d - 1],
                device_id={"col": to},
                device_id_type=MESH,
            )
            copy.start()
            copies.append(copy)
        return copies

    def finish(part, copies):
        start, size = parts[part]
        for copy in copies:
            copy.wait()
        total = zsend[part][col].astype(F32)
        for d in range(1, n_col):
            total += zrecv[part][d - 1].astype(F32)
        out_ref[start : start + size, :] = total

    translate(0)
    collect(0)
    pair0 = pair_start(0)
    translate(1)
    sends0 = spread_start(0, pair0)
    collect(1)
    pair1 = pair_start(1)
    sends1 = spread_start(1, pair1)
    finish(0, sends0)
    finish(1, sends1)


def iota(shape, axis):
    return lax.broadcasted_iota(jnp.int32, shape, axis)


def mirror(spot, half):
    upper = (spot >= half).astype(jnp.int32)
    within = spot - upper * half
    return (within >> 2) * 8 + upper * 4 + (within & 3)


def folded_kernel(
    dims,
    mult_hbm,
    op_hbm,
    cls_hbm,
    own_hbm,
    sep_ref,
    out_ref,
    gath,
    mult,
    ops,
    cls,
    own,
    pick,
    moved,
    place,
    acc,
    psend,
    precv,
    zsend,
    zrecv,
    local_sem,
    g_send,
    g_recv,
    p_send,
    p_recv,
    z_send,
    z_recv,
):
    n_row, n_col, n_core, parts = dims
    rows, width = mult_hbm.shape
    count = op_hbm.shape[0]
    targets, sources = cls_hbm.shape
    slots = out_ref.shape[1]
    group = n_col * n_core
    half = sources // 2
    row = lax.axis_index("row")
    col = lax.axis_index("col")
    core = lax.axis_index("cores")

    barrier = pltpu.get_barrier_semaphore()
    for d in range(1, n_row):
        pl.semaphore_signal(
            barrier, inc=1, device_id={"row": lax.rem(row + d, n_row)}, device_id_type=MESH
        )
    pl.semaphore_signal(barrier, inc=1, device_id={"cores": 1 - core}, device_id_type=MESH)
    for d in range(1, n_col):
        pl.semaphore_signal(
            barrier, inc=1, device_id={"col": lax.rem(col + d, n_col)}, device_id_type=MESH
        )

    cls_copy = pltpu.make_async_copy(cls_hbm, cls, local_sem.at[0])
    own_copy = pltpu.make_async_copy(own_hbm, own, local_sem.at[1])
    mine_copy = pltpu.make_async_copy(mult_hbm, gath.at[row], local_sem.at[2])
    op_copy = pltpu.make_async_copy(op_hbm, ops, local_sem.at[3])
    for copy in (cls_copy, own_copy, mine_copy, op_copy):
        copy.start()

    pl.semaphore_wait(barrier, n_row - 1 + n_col - 1 + 1)

    def beside(dy, dx):
        return lax.rem(row // 2 + dy, 2) * 2 + lax.rem(lax.rem(row, 2) + dx, 2)

    gathers = []
    for d, (dy, dx) in enumerate(((0, 1), (1, 0), (1, 1))):
        copy = pltpu.make_async_remote_copy(
            src_ref=mult_hbm,
            dst_ref=gath.at[row],
            send_sem=g_send.at[d],
            recv_sem=g_recv.at[d],
            device_id={"row": beside(dy, dx)},
            device_id_type=MESH,
        )
        copy.start()
        gathers.append(copy)

    cls_copy.wait()
    step = 2 * width
    lead = row // 2
    square = (sources, sources)
    swap = jnp.where(
        mirror(iota(square, 0), half) == iota(square, 1), 1.0, 0.0
    ).astype(BF16)
    spot = iota(square, 0)
    upper = (spot >= half).astype(jnp.int32)
    spot = spot - upper * half
    small = width // 2
    spot, base = (
        jnp.where(
            spot < small, spot, jnp.where(spot < width, spot - small, spot - width)
        ),
        jnp.where(
            spot < small,
            row * width,
            jnp.where(spot < width, beside(0, 1) * width, lax.rem(lead + 1, 2) * step),
        ),
    )
    turn = jnp.where(
        base + (spot >> 2) * 8 + upper * 4 + (spot & 3) == iota(square, 1), 1.0, 0.0
    ).astype(BF16)
    chosen = jnp.dot(
        swap[:half], cls[...].astype(F32).astype(BF16), preferred_element_type=F32
    ).astype(BF16)
    turned = lax.dot_general(
        turn, chosen, (((1,), (1,)), ((), ())), preferred_element_type=F32
    )
    flag = sep_ref[0, 0].astype(F32)
    wanted = ((turned - (core * count).astype(F32)) * flag + (flag - 1.0)).astype(BF16)
    chunks = (
        (0, 0, small),
        (count * small, small, small),
        (count * width, width, width),
    )
    one, zero = jnp.array(0.5, BF16), jnp.array(0.0, BF16)
    @pl.loop(0, count, unroll=10)
    def _(k):
        kind = jnp.asarray(k, F32).astype(BF16)
        same = jnp.where(wanted[0:half] == kind, one, zero)
        other = jnp.where(wanted[half:] == kind, one, zero)
        for which, both in enumerate((same + other, same - other)):
            for at, first, size in chunks:
                to = pl.multiple_of(at + k * size, size)
                pick[which, pl.ds(to, size), :] = both[first : first + size]

    own_copy.wait()
    owners = own[...]
    ids = iota((group, targets), 0)
    hit = jnp.where(ids == owners, 1.0, 0.0)
    upper = jnp.where(
        iota((targets, targets), 0) < iota((targets, targets), 1), 1.0, 0.0
    ).astype(BF16)
    before = jnp.dot(hit.astype(BF16), upper, preferred_element_type=F32)
    rank = jnp.sum(before * hit, axis=0, keepdims=True)
    both = jnp.where(ids == 0, owners.astype(F32), rank).astype(BF16)
    both = lax.dot_general(both, swap, (((1,), (1,)), ((), ())), preferred_element_type=F32)
    owners, rank = both[0:1], both[1:2]
    slot = iota((slots, targets), 0).astype(F32)
    for c in range(n_col):
        wants = jnp.where(owners == (c * n_core + core).astype(F32), rank, -1.0)
        place[:, c * slots : (c + 1) * slots] = jnp.where(slot == wants, 1.0, 0.0).T.astype(BF16)

    def arrange(at, many):
        wide = many * width
        order = jnp.where(
            mirror(iota((wide, wide), 1), wide // 2) == iota((wide, wide), 0), 1.0, 0.0
        ).astype(BF16)
        cells = [gath[at + i] for i in range(many)]
        cells = cells[0] if many == 1 else jnp.concatenate(cells, axis=1)
        return jnp.dot(cells, order, preferred_element_type=F32).astype(BF16)

    left = iota((1, width), 1) < small

    def translate_one(which, cells):
        for k in range(0, count, 2):
            got = [
                jnp.dot(ops[k + i], cells, preferred_element_type=F32).astype(BF16)
                for i in range(2)
            ]
            back = [pltpu.roll(g, small, 1) for g in got]
            at = (which * count + k) * small
            moved[0, 0:rows, at : at + width] = jnp.where(
                left, got[0] + back[0], got[1] + back[1]
            )
            moved[1, 0:rows, at : at + width] = jnp.where(
                left, got[0] - back[0], back[1] - got[1]
            )

    def fold(got, start, size, c, k):
        low, high = got[:, :width], got[:, width:]
        at = (c * count + k) * width
        moved[0, start : start + size, at : at + width] = low + high
        moved[1, start : start + size, at : at + width] = low - high

    def translate(start, size):
        c = 1
        if size % 16 == 0:
            many = ops[:, start : start + size, :].reshape(count * size, rows)
            got = jnp.dot(many, mult[...], preferred_element_type=F32).astype(BF16)
            for k in range(count):
                fold(got[k * size : (k + 1) * size], start, size, c, k)
        else:
            for k in range(count):
                got = jnp.dot(
                    ops[k, start : start + size, :], mult[...], preferred_element_type=F32
                ).astype(BF16)
                fold(got, start, size, c, k)

    def collect(part):
        start, size = parts[part]
        size = (size + 15) // 16 * 16
        begin = count * small
        for which in range(2):
            acc[which, start : start + size] += jnp.dot(
                moved[which, start : start + size, begin:],
                pick[which, begin:, :],
                preferred_element_type=F32,
            )
        even, odd = acc[0, start : start + size], acc[1, start : start + size]
        psend[start : start + size, :half] = even + odd
        psend[start : start + size, half:] = even - odd
        copy = pltpu.make_async_remote_copy(
            src_ref=psend.at[pl.ds(start, size)],
            dst_ref=precv.at[pl.ds(start, size)],
            send_sem=p_send.at[part],
            recv_sem=p_recv.at[part],
            device_id={"cores": 1 - core},
            device_id_type=MESH,
        )
        copy.start()
        return copy

    def spread(part, pair):
        start, size = parts[part]
        size = (size + 15) // 16 * 16
        pair.wait()
        total = (psend[start : start + size] + precv[start : start + size]).astype(BF16)
        placed = jnp.dot(total, place[...], preferred_element_type=F32).astype(BF16)
        for c in range(n_col):
            zsend[c, start : start + size] = placed[:, c * slots : (c + 1) * slots]
        copies = []
        for i in range(1, n_col):
            d = jnp.where(col < n_col // 2, n_col - i, i)
            to = lax.rem(col + d, n_col)
            copy = pltpu.make_async_remote_copy(
                src_ref=zsend.at[to, pl.ds(start, size)],
                dst_ref=zrecv.at[d - 1, pl.ds(start, size)],
                send_sem=z_send.at[part, d - 1],
                recv_sem=z_recv.at[part, d - 1],
                device_id={"col": to},
                device_id_type=MESH,
            )
            copy.start()
            copies.append(copy)
        return copies

    def finish(part, copies):
        start, size = parts[part]
        for copy in copies:
            copy.wait()
        total = zsend[col, start : start + size].astype(F32)
        for d in range(1, n_col):
            total += zrecv[d - 1, start : start + size].astype(F32)
        out_ref[start : start + size, :] = total

    mine_copy.wait()
    cells = arrange(row, 1)
    op_copy.wait()
    translate_one(0, cells)
    for which in range(2):
        acc[which] = jnp.dot(
            moved[which, :, : count * small],
            pick[which, : count * small, :],
            preferred_element_type=F32,
        )
    gathers[0].wait()
    translate_one(1, arrange(beside(0, 1), 1))
    gathers[1].wait()
    gathers[2].wait()
    mult[...] = arrange(2 * lax.rem(lead + 1, 2), 2)
    pairs, sends = [], []
    for part in range(len(parts)):
        translate(*parts[part])
        if part > 0:
            sends.append(spread(part - 1, pairs[part - 1]))
        pairs.append(collect(part))
    sends.append(spread(len(parts) - 1, pairs[-1]))
    for part in range(len(parts)):
        finish(part, sends[part])


def folded(mesh, multipoles, operators, classes, separated, owners):
    n_row, n_col, n_core = mesh.shape["row"], mesh.shape["col"], mesh.shape["cores"]
    rows, width = multipoles.shape
    count = operators.shape[0]
    targets, sources = classes.shape
    slots = 2 * targets // (n_col * n_core)
    cuts = [0, *CUTS, rows]
    parts = tuple((at, to - at) for at, to in zip(cuts, cuts[1:]))
    n, top = len(parts), (rows + 15) // 16 * 16
    hbm = pl.BlockSpec(memory_space=pltpu.HBM)
    dma = pltpu.SemaphoreType.DMA
    operands = [
        pltpu.with_memory_space_constraint(x, pltpu.HBM)
        for x in (multipoles, operators, classes, owners.reshape(1, targets))
    ]
    return pl.pallas_call(
        functools.partial(folded_kernel, (n_row, n_col, n_core, parts)),
        out_shape=jax.ShapeDtypeStruct((rows, slots), F32),
        in_specs=[hbm] * 4 + [pl.BlockSpec(memory_space=pltpu.SMEM)],
        out_specs=pl.BlockSpec(memory_space=pltpu.VMEM),
        scratch_shapes=[
            pltpu.VMEM((n_row, rows, width), BF16),
            pltpu.VMEM((rows, 2 * width), BF16),
            pltpu.VMEM((count, rows, rows), BF16),
            pltpu.VMEM((targets, sources), jnp.int32),
            pltpu.VMEM((1, targets), jnp.int32),
            pltpu.VMEM((2, count * sources // 2, targets // 2), BF16),
            pltpu.VMEM((2, top, count * sources // 2), BF16),
            pltpu.VMEM((targets, n_col * slots), BF16),
            pltpu.VMEM((2, top, targets // 2), F32),
            pltpu.VMEM((top, targets), F32),
            pltpu.VMEM((top, targets), F32),
            pltpu.VMEM((n_col, top, slots), BF16),
            pltpu.VMEM((n_col - 1, top, slots), BF16),
            dma((4,)),
            dma((n_row - 1,)),
            dma((n_row - 1,)),
            dma((n,)),
            dma((n,)),
            dma((n, n_col - 1)),
            dma((n, n_col - 1)),
        ],
        compiler_params=pltpu.CompilerParams(
            collective_id=0, has_side_effects=True, vmem_limit_bytes=44 * 1024 * 1024
        ),
    )(*operands, separated)


def solution(mesh):
    n_row, n_col, n_core = mesh.shape["row"], mesh.shape["col"], mesh.shape["cores"]

    def shards(multipoles, operators, classes, separated, owners):
        rows, width = multipoles.shape
        count = operators.shape[0]
        targets, sources = classes.shape
        slots = 2 * targets // (n_col * n_core)
        if separated.shape[1] == 1 and n_row == 4 and n_core == 2 and width % 128 == 0:
            return folded(mesh, multipoles, operators, classes, separated, owners)
        sizes = [size for _, size in split_rows(rows)]
        top = sizes[0] * 2
        hbm = pl.BlockSpec(memory_space=pl.ANY)
        dma = pltpu.SemaphoreType.DMA
        return pl.pallas_call(
            functools.partial(kernel, (n_row, n_col, n_core, separated.shape[1])),
            out_shape=jax.ShapeDtypeStruct((rows, slots), F32),
            in_specs=[
                hbm,
                hbm,
                hbm,
                pl.BlockSpec(memory_space=pltpu.SMEM),
                pl.BlockSpec(memory_space=pltpu.VMEM),
            ],
            out_specs=pl.BlockSpec(memory_space=pltpu.VMEM),
            scratch_shapes=[
                pltpu.VMEM((n_row, rows, width), BF16),
                pltpu.VMEM((rows, sources), BF16),
                pltpu.VMEM((count, rows, rows), BF16),
                pltpu.VMEM((targets, sources), jnp.int32),
                pltpu.VMEM((count * sources, targets), BF16),
                pltpu.VMEM((top, count * sources), BF16),
                pltpu.VMEM((sizes[0], targets), F32),
                pltpu.VMEM((targets, n_col * slots), BF16),
            ]
            + [pltpu.VMEM((size, targets), BF16) for size in sizes]
            + [pltpu.VMEM((size, targets), BF16) for size in sizes]
            + [pltpu.VMEM((n_col, size, slots), BF16) for size in sizes]
            + [pltpu.VMEM((n_col - 1, size, slots), BF16) for size in sizes]
            + [
                dma((3,)),
                dma((n_row - 1,)),
                dma((n_row - 1,)),
                dma((2,)),
                dma((2,)),
                dma((2, n_col - 1)),
                dma((2, n_col - 1)),
            ],
            compiler_params=pltpu.CompilerParams(
                collective_id=0, has_side_effects=True, vmem_limit_bytes=60 * 1024 * 1024
            ),
        )(multipoles, operators, classes, separated, owners.reshape(1, targets))

    return jax.shard_map(
        shards,
        mesh=mesh,
        in_specs=(
            P(None, ("col", "row")),
            P("cores", None, None),
            P("row", "col"),
            P("row", "col"),
            P("row"),
        ),
        out_specs=P(None, ("row", "col", "cores")),
        check_vma=False,
    )
```

```python
import functools

import jax
import jax.numpy as jnp
from jax import lax
from jax.experimental import pallas as pl
from jax.experimental.pallas import tpu as pltpu
from jax.sharding import PartitionSpec as P

MESH = pl.DeviceIdType.MESH
F32 = jnp.float32
BF16 = jnp.bfloat16
CUTS = (96, 208)


def split_rows(rows):
    first = (rows // 2 + 15) // 16 * 16
    return ((0, first), (first, rows - first))


def kernel(
    dims,
    mult_hbm,
    op_hbm,
    cls_hbm,
    sep_ref,
    own_ref,
    out_ref,
    gath,
    mult,
    ops,
    cls,
    pick,
    moved,
    acc,
    place,
    psend0,
    psend1,
    precv0,
    precv1,
    zsend0,
    zsend1,
    zrecv0,
    zrecv1,
    local_sem,
    g_send,
    g_recv,
    p_send,
    p_recv,
    z_send,
    z_recv,
):
    n_row, n_col, n_core, spread = dims
    rows, width = mult_hbm.shape
    count = op_hbm.shape[0]
    targets, sources = cls_hbm.shape
    slots = zsend0.shape[2]
    group = n_col * n_core
    row = lax.axis_index("row")
    col = lax.axis_index("col")
    core = lax.axis_index("cores")
    parts = split_rows(rows)
    psend, precv = (psend0, psend1), (precv0, precv1)
    zsend, zrecv = (zsend0, zsend1), (zrecv0, zrecv1)

    barrier = pltpu.get_barrier_semaphore()
    for d in range(1, n_row):
        pl.semaphore_signal(
            barrier, inc=1, device_id={"row": lax.rem(row + d, n_row)}, device_id_type=MESH
        )
    for d in range(1, n_col):
        pl.semaphore_signal(
            barrier, inc=1, device_id={"col": lax.rem(col + d, n_col)}, device_id_type=MESH
        )
    pl.semaphore_signal(barrier, inc=1, device_id={"cores": 1 - core}, device_id_type=MESH)

    cls_copy = pltpu.make_async_copy(cls_hbm, cls, local_sem.at[0])
    cls_copy.start()
    own_copy = pltpu.make_async_copy(mult_hbm, gath.at[row], local_sem.at[1])
    own_copy.start()
    op_copy = pltpu.make_async_copy(op_hbm, ops, local_sem.at[2])
    op_copy.start()

    pl.semaphore_wait(barrier, n_row - 1 + n_col - 1 + 1)

    gathers = []
    for d in range(1, n_row):
        copy = pltpu.make_async_remote_copy(
            src_ref=mult_hbm,
            dst_ref=gath.at[row],
            send_sem=g_send.at[d - 1],
            recv_sem=g_recv.at[d - 1],
            device_id={"row": lax.rem(row + d, n_row)},
            device_id_type=MESH,
        )
        copy.start()
        gathers.append(copy)

    cls_copy.wait()
    per = sources // spread
    for j in range(spread):
        flag = sep_ref[0, j]
        block = cls[:, j * per : (j + 1) * per]
        wanted = (block - core * count) * flag + (flag - 1)
        turned = wanted.astype(F32).T
        for k in range(count):
            pick[pl.ds(k * sources + j * per, per), :] = jnp.where(
                turned == float(k), 1.0, 0.0
            ).astype(BF16)

    owners = own_ref[...]
    ids = lax.broadcasted_iota(jnp.int32, (group, targets), 0)
    hit = jnp.where(ids == owners, 1.0, 0.0)
    upper = jnp.where(
        lax.broadcasted_iota(jnp.int32, (targets, targets), 0)
        < lax.broadcasted_iota(jnp.int32, (targets, targets), 1),
        1.0,
        0.0,
    ).astype(BF16)
    before = jnp.dot(hit.astype(BF16), upper, preferred_element_type=F32)
    rank = jnp.sum(before * hit, axis=0, keepdims=True)
    slot = lax.broadcasted_iota(jnp.int32, (slots, targets), 0).astype(F32)
    for c in range(n_col):
        mine = jnp.where(owners == c * n_core + core, rank, -1.0)
        place[:, c * slots : (c + 1) * slots] = jnp.where(slot == mine, 1.0, 0.0).T.astype(BF16)

    own_copy.wait()
    for copy in gathers:
        copy.wait()
    if width % 128 == 0:
        for r in range(n_row):
            mult[:, r * width : (r + 1) * width] = gath[r]
    else:
        mult[...] = jnp.concatenate([gath[r] for r in range(n_row)], axis=1)
    op_copy.wait()

    def translate(part):
        start, size = parts[part]

        @pl.loop(0, count, unroll=20)
        def _(k):
            at = pl.multiple_of(k * sources, sources)
            moved[part * parts[0][1] : part * parts[0][1] + size, pl.ds(at, sources)] = jnp.dot(
                ops[k, start : start + size, :], mult[...], preferred_element_type=F32
            ).astype(BF16)

    def collect(part):
        start, size = parts[part]
        chunk = 10 if count % 10 == 0 else 1
        acc[0:size, :] = jnp.zeros((size, targets), F32)

        @pl.loop(0, count // chunk)
        def _(g):
            at = pl.multiple_of(g * chunk * sources, chunk * sources)
            acc[0:size, :] += jnp.dot(
                moved[part * parts[0][1] : part * parts[0][1] + size, pl.ds(at, chunk * sources)],
                pick[pl.ds(at, chunk * sources), :],
                preferred_element_type=F32,
            )

    def pair_start(part):
        size = parts[part][1]
        psend[part][...] = acc[0:size, :].astype(BF16)
        copy = pltpu.make_async_remote_copy(
            src_ref=psend[part],
            dst_ref=precv[part],
            send_sem=p_send.at[part],
            recv_sem=p_recv.at[part],
            device_id={"cores": 1 - core},
            device_id_type=MESH,
        )
        copy.start()
        return copy

    def spread_start(part, pair):
        size = parts[part][1]
        pair.wait()
        both = (psend[part][...].astype(F32) + precv[part][...].astype(F32)).astype(BF16)
        if slots % 128 == 0:
            placed = jnp.dot(both, place[...], preferred_element_type=F32).astype(BF16)
            for c in range(n_col):
                zsend[part][c] = placed[:, c * slots : (c + 1) * slots]
        else:
            for c in range(n_col):
                zsend[part][c] = jnp.dot(
                    both, place[:, c * slots : (c + 1) * slots], preferred_element_type=F32
                ).astype(BF16)
        copies = []
        for d in range(1, n_col):
            to = lax.rem(col + d, n_col)
            copy = pltpu.make_async_remote_copy(
                src_ref=zsend[part].at[to],
                dst_ref=zrecv[part].at[d - 1],
                send_sem=z_send.at[part, d - 1],
                recv_sem=z_recv.at[part, d - 1],
                device_id={"col": to},
                device_id_type=MESH,
            )
            copy.start()
            copies.append(copy)
        return copies

    def finish(part, copies):
        start, size = parts[part]
        for copy in copies:
            copy.wait()
        total = zsend[part][col].astype(F32)
        for d in range(1, n_col):
            total += zrecv[part][d - 1].astype(F32)
        out_ref[start : start + size, :] = total

    translate(0)
    collect(0)
    pair0 = pair_start(0)
    translate(1)
    sends0 = spread_start(0, pair0)
    collect(1)
    pair1 = pair_start(1)
    sends1 = spread_start(1, pair1)
    finish(0, sends0)
    finish(1, sends1)


def iota(shape, axis):
    return lax.broadcasted_iota(jnp.int32, shape, axis)


def mirror(spot, half):
    upper = (spot >= half).astype(jnp.int32)
    within = spot - upper * half
    return (within >> 2) * 8 + upper * 4 + (within & 3)


def folded_kernel(
    dims,
    mult_hbm,
    op_hbm,
    cls_hbm,
    own_hbm,
    sep_ref,
    out_ref,
    gath,
    mult,
    ops,
    cls,
    own,
    pick,
    moved,
    place,
    acc,
    psend,
    precv,
    zsend,
    zrecv,
    local_sem,
    g_send,
    g_recv,
    p_send,
    p_recv,
    z_send,
    z_recv,
):
    n_row, n_col, n_core, parts = dims
    rows, width = mult_hbm.shape
    count = op_hbm.shape[0]
    targets, sources = cls_hbm.shape
    slots = out_ref.shape[1]
    group = n_col * n_core
    half = sources // 2
    row = lax.axis_index("row")
    col = lax.axis_index("col")
    core = lax.axis_index("cores")

    barrier = pltpu.get_barrier_semaphore()
    for d in range(1, n_row):
        pl.semaphore_signal(
            barrier, inc=1, device_id={"row": lax.rem(row + d, n_row)}, device_id_type=MESH
        )
    pl.semaphore_signal(barrier, inc=1, device_id={"cores": 1 - core}, device_id_type=MESH)
    for d in range(1, n_col):
        pl.semaphore_signal(
            barrier, inc=1, device_id={"col": lax.rem(col + d, n_col)}, device_id_type=MESH
        )

    cls_copy = pltpu.make_async_copy(cls_hbm, cls, local_sem.at[0])
    own_copy = pltpu.make_async_copy(own_hbm, own, local_sem.at[1])
    mine_copy = pltpu.make_async_copy(mult_hbm, gath.at[row], local_sem.at[2])
    op_copy = pltpu.make_async_copy(op_hbm, ops, local_sem.at[3])
    for copy in (cls_copy, own_copy, mine_copy, op_copy):
        copy.start()

    pl.semaphore_wait(barrier, n_row - 1 + n_col - 1 + 1)

    def beside(dy, dx):
        return lax.rem(row // 2 + dy, 2) * 2 + lax.rem(lax.rem(row, 2) + dx, 2)

    gathers = []
    for d, (dy, dx) in enumerate(((0, 1), (1, 0), (1, 1))):
        copy = pltpu.make_async_remote_copy(
            src_ref=mult_hbm,
            dst_ref=gath.at[row],
            send_sem=g_send.at[d],
            recv_sem=g_recv.at[d],
            device_id={"row": beside(dy, dx)},
            device_id_type=MESH,
        )
        copy.start()
        gathers.append(copy)

    cls_copy.wait()
    step = 2 * width
    lead = row // 2
    square = (sources, sources)
    swap = jnp.where(
        mirror(iota(square, 0), half) == iota(square, 1), 1.0, 0.0
    ).astype(BF16)
    spot = iota(square, 0)
    upper = (spot >= half).astype(jnp.int32)
    spot = spot - upper * half
    small = width // 2
    spot, base = (
        jnp.where(
            spot < small, spot, jnp.where(spot < width, spot - small, spot - width)
        ),
        jnp.where(
            spot < small,
            row * width,
            jnp.where(spot < width, beside(0, 1) * width, lax.rem(lead + 1, 2) * step),
        ),
    )
    turn = jnp.where(
        base + (spot >> 2) * 8 + upper * 4 + (spot & 3) == iota(square, 1), 1.0, 0.0
    ).astype(BF16)
    chosen = jnp.dot(
        swap[:half], cls[...].astype(F32).astype(BF16), preferred_element_type=F32
    ).astype(BF16)
    turned = lax.dot_general(
        turn, chosen, (((1,), (1,)), ((), ())), preferred_element_type=F32
    )
    flag = sep_ref[0, 0].astype(F32)
    wanted = ((turned - (core * count).astype(F32)) * flag + (flag - 1.0)).astype(BF16)
    chunks = (
        (0, 0, small),
        (count * small, small, small),
        (count * width, width, width),
    )
    one, zero = jnp.array(0.5, BF16), jnp.array(0.0, BF16)
    @pl.loop(0, count, unroll=20)
    def _(k):
        kind = jnp.asarray(k, F32).astype(BF16)
        same = jnp.where(wanted[0:half] == kind, one, zero)
        other = jnp.where(wanted[half:] == kind, one, zero)
        for which, both in enumerate((same + other, same - other)):
            for at, first, size in chunks:
                to = pl.multiple_of(at + k * size, size)
                pick[which, pl.ds(to, size), :] = both[first : first + size]

    own_copy.wait()
    owners = own[...]
    ids = iota((group, targets), 0)
    hit = jnp.where(ids == owners, 1.0, 0.0)
    upper = jnp.where(
        iota((targets, targets), 0) < iota((targets, targets), 1), 1.0, 0.0
    ).astype(BF16)
    before = jnp.dot(hit.astype(BF16), upper, preferred_element_type=F32)
    rank = jnp.sum(before * hit, axis=0, keepdims=True)
    both = jnp.where(ids == 0, owners.astype(F32), rank).astype(BF16)
    both = lax.dot_general(both, swap, (((1,), (1,)), ((), ())), preferred_element_type=F32)
    owners, rank = both[0:1], both[1:2]
    slot = iota((slots, targets), 0).astype(F32)
    for c in range(n_col):
        wants = jnp.where(owners == (c * n_core + core).astype(F32), rank, -1.0)
        place[:, c * slots : (c + 1) * slots] = jnp.where(slot == wants, 1.0, 0.0).T.astype(BF16)

    def arrange(at, many):
        wide = many * width
        order = jnp.where(
            mirror(iota((wide, wide), 1), wide // 2) == iota((wide, wide), 0), 1.0, 0.0
        ).astype(BF16)
        cells = [gath[at + i] for i in range(many)]
        cells = cells[0] if many == 1 else jnp.concatenate(cells, axis=1)
        return jnp.dot(cells, order, preferred_element_type=F32).astype(BF16)

    left = iota((1, width), 1) < small

    def translate_one(which, cells):
        for k in range(0, count, 2):
            got = [
                jnp.dot(ops[k + i], cells, preferred_element_type=F32).astype(BF16)
                for i in range(2)
            ]
            back = [pltpu.roll(g, small, 1) for g in got]
            at = (which * count + k) * small
            moved[0, 0:rows, at : at + width] = jnp.where(
                left, got[0] + back[0], got[1] + back[1]
            )
            moved[1, 0:rows, at : at + width] = jnp.where(
                left, got[0] - back[0], back[1] - got[1]
            )

    def fold(got, start, size, c, k):
        low, high = got[:, :width], got[:, width:]
        at = (c * count + k) * width
        moved[0, start : start + size, at : at + width] = low + high
        moved[1, start : start + size, at : at + width] = low - high

    def translate(start, size):
        c = 1
        if size % 16 == 0:
            many = ops[:, start : start + size, :].reshape(count * size, rows)
            got = jnp.dot(many, mult[...], preferred_element_type=F32).astype(BF16)
            for k in range(count):
                fold(got[k * size : (k + 1) * size], start, size, c, k)
        else:
            for k in range(count):
                got = jnp.dot(
                    ops[k, start : start + size, :], mult[...], preferred_element_type=F32
                ).astype(BF16)
                fold(got, start, size, c, k)

    def collect(part):
        start, size = parts[part]
        size = (size + 15) // 16 * 16
        begin = count * small
        for which in range(2):
            acc[which, start : start + size] += jnp.dot(
                moved[which, start : start + size, begin:],
                pick[which, begin:, :],
                preferred_element_type=F32,
            )
        even, odd = acc[0, start : start + size], acc[1, start : start + size]
        psend[start : start + size, :half] = even + odd
        psend[start : start + size, half:] = even - odd
        copy = pltpu.make_async_remote_copy(
            src_ref=psend.at[pl.ds(start, size)],
            dst_ref=precv.at[pl.ds(start, size)],
            send_sem=p_send.at[part],
            recv_sem=p_recv.at[part],
            device_id={"cores": 1 - core},
            device_id_type=MESH,
        )
        copy.start()
        return copy

    def spread(part, pair):
        start, size = parts[part]
        size = (size + 15) // 16 * 16
        pair.wait()
        total = (psend[start : start + size] + precv[start : start + size]).astype(BF16)
        placed = jnp.dot(total, place[...], preferred_element_type=F32).astype(BF16)
        for c in range(n_col):
            zsend[c, start : start + size] = placed[:, c * slots : (c + 1) * slots]
        copies = []
        for i in range(1, n_col):
            d = jnp.where(col < n_col // 2, n_col - i, i)
            to = lax.rem(col + d, n_col)
            copy = pltpu.make_async_remote_copy(
                src_ref=zsend.at[to, pl.ds(start, size)],
                dst_ref=zrecv.at[d - 1, pl.ds(start, size)],
                send_sem=z_send.at[part, d - 1],
                recv_sem=z_recv.at[part, d - 1],
                device_id={"col": to},
                device_id_type=MESH,
            )
            copy.start()
            copies.append(copy)
        return copies

    def finish(part, copies):
        start, size = parts[part]
        for copy in copies:
            copy.wait()
        total = zsend[col, start : start + size].astype(F32)
        for d in range(1, n_col):
            total += zrecv[d - 1, start : start + size].astype(F32)
        out_ref[start : start + size, :] = total

    mine_copy.wait()
    cells = arrange(row, 1)
    op_copy.wait()
    translate_one(0, cells)
    for which in range(2):
        acc[which] = jnp.dot(
            moved[which, :, : count * small],
            pick[which, : count * small, :],
            preferred_element_type=F32,
        )
    gathers[0].wait()
    translate_one(1, arrange(beside(0, 1), 1))
    gathers[1].wait()
    gathers[2].wait()
    mult[...] = arrange(2 * lax.rem(lead + 1, 2), 2)
    pairs, sends = [], []
    for part in range(len(parts)):
        translate(*parts[part])
        if part > 0:
            sends.append(spread(part - 1, pairs[part - 1]))
        pairs.append(collect(part))
    sends.append(spread(len(parts) - 1, pairs[-1]))
    for part in range(len(parts)):
        finish(part, sends[part])


def folded(mesh, multipoles, operators, classes, separated, owners):
    n_row, n_col, n_core = mesh.shape["row"], mesh.shape["col"], mesh.shape["cores"]
    rows, width = multipoles.shape
    count = operators.shape[0]
    targets, sources = classes.shape
    slots = 2 * targets // (n_col * n_core)
    cuts = [0, *CUTS, rows]
    parts = tuple((at, to - at) for at, to in zip(cuts, cuts[1:]))
    n, top = len(parts), (rows + 15) // 16 * 16
    hbm = pl.BlockSpec(memory_space=pltpu.HBM)
    dma = pltpu.SemaphoreType.DMA
    operands = [
        pltpu.with_memory_space_constraint(x, pltpu.HBM)
        for x in (multipoles, operators, classes, owners.reshape(1, targets))
    ]
    return pl.pallas_call(
        functools.partial(folded_kernel, (n_row, n_col, n_core, parts)),
        out_shape=jax.ShapeDtypeStruct((rows, slots), F32),
        in_specs=[hbm] * 4 + [pl.BlockSpec(memory_space=pltpu.SMEM)],
        out_specs=pl.BlockSpec(memory_space=pltpu.VMEM),
        scratch_shapes=[
            pltpu.VMEM((n_row, rows, width), BF16),
            pltpu.VMEM((rows, 2 * width), BF16),
            pltpu.VMEM((count, rows, rows), BF16),
            pltpu.VMEM((targets, sources), jnp.int32),
            pltpu.VMEM((1, targets), jnp.int32),
            pltpu.VMEM((2, count * sources // 2, targets // 2), BF16),
            pltpu.VMEM((2, top, count * sources // 2), BF16),
            pltpu.VMEM((targets, n_col * slots), BF16),
            pltpu.VMEM((2, top, targets // 2), F32),
            pltpu.VMEM((top, targets), F32),
            pltpu.VMEM((top, targets), F32),
            pltpu.VMEM((n_col, top, slots), BF16),
            pltpu.VMEM((n_col - 1, top, slots), BF16),
            dma((4,)),
            dma((n_row - 1,)),
            dma((n_row - 1,)),
            dma((n,)),
            dma((n,)),
            dma((n, n_col - 1)),
            dma((n, n_col - 1)),
        ],
        compiler_params=pltpu.CompilerParams(
            collective_id=0, has_side_effects=True, vmem_limit_bytes=44 * 1024 * 1024
        ),
    )(*operands, separated)


def solution(mesh):
    n_row, n_col, n_core = mesh.shape["row"], mesh.shape["col"], mesh.shape["cores"]

    def shards(multipoles, operators, classes, separated, owners):
        rows, width = multipoles.shape
        count = operators.shape[0]
        targets, sources = classes.shape
        slots = 2 * targets // (n_col * n_core)
        if separated.shape[1] == 1 and n_row == 4 and n_core == 2 and width % 128 == 0:
            return folded(mesh, multipoles, operators, classes, separated, owners)
        sizes = [size for _, size in split_rows(rows)]
        top = sizes[0] * 2
        hbm = pl.BlockSpec(memory_space=pl.ANY)
        dma = pltpu.SemaphoreType.DMA
        return pl.pallas_call(
            functools.partial(kernel, (n_row, n_col, n_core, separated.shape[1])),
            out_shape=jax.ShapeDtypeStruct((rows, slots), F32),
            in_specs=[
                hbm,
                hbm,
                hbm,
                pl.BlockSpec(memory_space=pltpu.SMEM),
                pl.BlockSpec(memory_space=pltpu.VMEM),
            ],
            out_specs=pl.BlockSpec(memory_space=pltpu.VMEM),
            scratch_shapes=[
                pltpu.VMEM((n_row, rows, width), BF16),
                pltpu.VMEM((rows, sources), BF16),
                pltpu.VMEM((count, rows, rows), BF16),
                pltpu.VMEM((targets, sources), jnp.int32),
                pltpu.VMEM((count * sources, targets), BF16),
                pltpu.VMEM((top, count * sources), BF16),
                pltpu.VMEM((sizes[0], targets), F32),
                pltpu.VMEM((targets, n_col * slots), BF16),
            ]
            + [pltpu.VMEM((size, targets), BF16) for size in sizes]
            + [pltpu.VMEM((size, targets), BF16) for size in sizes]
            + [pltpu.VMEM((n_col, size, slots), BF16) for size in sizes]
            + [pltpu.VMEM((n_col - 1, size, slots), BF16) for size in sizes]
            + [
                dma((3,)),
                dma((n_row - 1,)),
                dma((n_row - 1,)),
                dma((2,)),
                dma((2,)),
                dma((2, n_col - 1)),
                dma((2, n_col - 1)),
            ],
            compiler_params=pltpu.CompilerParams(
                collective_id=0, has_side_effects=True, vmem_limit_bytes=60 * 1024 * 1024
            ),
        )(multipoles, operators, classes, separated, owners.reshape(1, targets))

    return jax.shard_map(
        shards,
        mesh=mesh,
        in_specs=(
            P(None, ("col", "row")),
            P("cores", None, None),
            P("row", "col"),
            P("row", "col"),
            P("row"),
        ),
        out_specs=P(None, ("row", "col", "cores")),
        check_vma=False,
    )
```
